32 devices in a mesh: shot: 2 (over y), gx: 4 (over z), gy: 4 (over x, core).
Axes of the slice: x: 2, y: 2, z: 4, core: 2. Of those that a mesh axis runs over, the one named last changes fastest.
Arguments:
- source_prev: float32 [64, 32, 320], P(('shot', 'gx'), 'gy'), parts along dimension 0, may hold values from -0.6 to 0.6
- source_now: float32 [64, 32, 320], P(('shot', 'gx'), 'gy'), parts along dimension 0, may hold values from -0.6 to 0.6
- receiver_prev: float32 [64, 32, 320], P(('shot', 'gx'), 'gy'), parts along dimension 0, may hold values from -6 to 6
- receiver_now: float32 [64, 32, 320], P(('shot', 'gx'), 'gy'), parts along dimension 0, may hold values from -6 to 6
- speed_squared: float32 [64, 32, 320], P(('shot', 'gx'), 'gy'), parts along dimension 0, may hold values from 0.05 to 0.18
- wavelet: float32 [20], P('shot'), parts along dimension 0, may hold values from -40 to 40
- source_cell: int32 [2], P('shot'), parts along dimension 0, may hold values from 0 to 327679
- traces: float32 [20, 1024], P('shot', ('gx', 'gy')), parts along dimension 0, may hold values from -18 to 18
- receiver_cells: int32 [2, 1024], P('shot', ('gx', 'gy')), parts along dimension 0, may hold values from 0 to 1023
- plan: int32 [8], P('shot'), parts along dimension 0, may hold values from 0 to 9, as said below
- stored_snapshots: bfloat16 [8, 32, 32, 320], P('shot', 'gx', 'gy'), parts along dimension 0, may hold values from -6 to 6
- image_before: float32 [64, 32, 320], P(('shot', 'gx'), 'gy'), parts along dimension 0, may hold values from -6 to 6
Outputs:
- new_source_prev: float32 [64, 32, 320], P(('shot', 'gx'), 'gy'), parts along dimension 0
- new_source_now: float32 [64, 32, 320], P(('shot', 'gx'), 'gy'), parts along dimension 0
- new_receiver_prev: float32 [64, 32, 320], P(('shot', 'gx'), 'gy'), parts along dimension 0
- new_receiver_now: float32 [64, 32, 320], P(('shot', 'gx'), 'gy'), parts along dimension 0
- snapshots: bfloat16 [8, 32, 32, 320], P('shot', 'gx', 'gy'), parts along dimension 0
- image: float32 [64, 32, 320], P(('shot', 'gx'), 'gy'), parts along dimension 0
The draws below stay inside these ranges and needn't reach their ends.
There are 2 independent parts, one for each index of `shot`. The reference program is written for one: setup_inputs(seed, part) draws one part's arguments, and reference() takes and returns one part's arrays. A program takes and returns all parts, laid end to end along the dimension named above; each array names one. Nothing has to cross between parts.
Inputs may be any that keep to these rules, and one draw needn't show every extreme that they name: `plan`: 4 different steps in increasing order; the first is 0 and the last is 9.
All inputs are finite; a program needn't handle non-finite values.
Results may differ from the reference program's by a relative error of at most 0.001.
Values sent between devices are 32-bit elements; how exact they have to be, the bound alone decides.
A program may use at most 64 MiB of HBM per device.

```python
import math
import jax
import jax.numpy as jnp
from jax import lax

NZ = 320
STEPS = 10
NSNAP = 4
NX = 32
NY = 32
NREC = 1024


def draw_plan(key, part):
    middle = jax.random.permutation(jax.random.fold_in(key, 11), STEPS - 2)[:NSNAP - 2] + 1
    middle = jnp.sort(middle.astype(jnp.int32))
    return jnp.concatenate([jnp.zeros((1,), jnp.int32), middle, jnp.full((1,), STEPS - 1, jnp.int32)])


def touch_ends(values, stream_key, least, largest):
    longest = values.shape.index(max(values.shape))
    spots = []
    for shift in (0, 1):
        where = [jax.random.randint(jax.random.fold_in(stream_key, axis), (), 0, length) for axis, length in enumerate(values.shape)]
        where[longest] = (where[longest] + shift) % values.shape[longest]
        spots.append(tuple(where))
    return values.at[spots[0]].set(least).at[spots[1]].set(largest)


def level_of(rng, shape, shards, low, high):
    level = 1.0
    for dim, blocks in shards:
        heights = jax.random.uniform(jax.random.fold_in(jax.random.fold_in(rng, 6), dim), (blocks,), jnp.float32, low / len(shards), high / len(shards))
        level = level * jnp.repeat(jnp.exp(heights), shape[dim] // blocks).reshape((-1,) + (1,) * (len(shape) - 1 - dim))
    return level


def normal_values(own_key, shape, deviation, most, cuts=(), kind=jnp.bfloat16):
    drawn = deviation * jax.random.normal(own_key, shape, jnp.float32)
    if cuts:
        drawn = drawn * level_of(own_key, shape, cuts, -0.22, 0.18)
    return jnp.clip(drawn, -most, most).astype(kind)


def setup_inputs(seed: int = 0, part: int = 0) -> dict:
    arg_keys = jax.random.split(jax.random.key(seed), 13)
    part_keys = jax.random.split(jax.random.fold_in(arg_keys[12], part), 13)
    source_prev = normal_values(part_keys[0], (NX, NY, NZ), 0.1, 0.6, ((0, 4), (1, 4)), jnp.float32)
    source_now = normal_values(part_keys[1], (NX, NY, NZ), 0.1, 0.6, ((0, 4), (1, 4)), jnp.float32)
    receiver_prev = normal_values(part_keys[2], (NX, NY, NZ), 1.0, 6.0, ((0, 4), (1, 4)), jnp.float32)
    receiver_now = normal_values(part_keys[3], (NX, NY, NZ), 1.0, 6.0, ((0, 4), (1, 4)), jnp.float32)
    speed_squared = jnp.clip(jnp.exp(math.log(0.18) - 1.2809339 * jax.random.uniform(part_keys[4], (NX, NY, NZ), jnp.float32) ** level_of(part_keys[4], (NX, NY, NZ), ((0, 4), (1, 4)), -0.2, 0.2)), 0.05, 0.18)
    wavelet = normal_values(part_keys[5], (STEPS,), 8.0, 40.0, (), jnp.float32)
    source_cell = jax.random.randint(part_keys[6], (1,), 0, NX * NY * NZ).astype(jnp.int32)
    traces = normal_values(part_keys[7], (STEPS, NREC), 3.0, 18.0, ((1, 16),), jnp.float32)
    receiver_cells = touch_ends(jax.random.randint(part_keys[8], (1, NREC), 0, NX * NY), jax.random.fold_in(part_keys[8], 1), 0, (NX * NY) - 1).astype(jnp.int32)
    plan = draw_plan(jax.random.fold_in(jax.random.fold_in(arg_keys[12], part), 71), part)
    stored_snapshots = normal_values(part_keys[10], (NSNAP, NX, NY, NZ), 1.0, 6.0, ((1, 4), (2, 4)))
    image_before = normal_values(part_keys[11], (NX, NY, NZ), 1.0, 6.0, ((0, 4), (1, 4)), jnp.float32)
    return {"source_prev": source_prev, "source_now": source_now, "receiver_prev": receiver_prev, "receiver_now": receiver_now, "speed_squared": speed_squared, "wavelet": wavelet, "source_cell": source_cell, "traces": traces, "receiver_cells": receiver_cells, "plan": plan, "stored_snapshots": stored_snapshots, "image_before": image_before}


STENCIL_COEFFS = (-205.0 / 72.0, 8.0 / 5.0, -1.0 / 5.0, 8.0 / 315.0, -1.0 / 560.0)


def stencil(padded):
    span_x = padded.shape[0] - 8
    span_y = padded.shape[1] - 8
    depth_cells = padded.shape[2]
    deepened = jnp.pad(padded, ((0, 0), (0, 0), (4, 4)))

    def window(shift_x, shift_y, shift_z):
        return deepened[4 + shift_x:4 + shift_x + span_x, 4 + shift_y:4 + shift_y + span_y,
                        4 + shift_z:4 + shift_z + depth_cells]

    summed = (3.0 * STENCIL_COEFFS[0]) * window(0, 0, 0)
    for distance in range(1, 5):
        neighbours = window(distance, 0, 0) + window(-distance, 0, 0)
        neighbours = neighbours + window(0, distance, 0) + window(0, -distance, 0)
        neighbours = neighbours + window(0, 0, distance) + window(0, 0, -distance)
        summed = summed + STENCIL_COEFFS[distance] * neighbours
    return summed


def reference(source_prev, source_now, receiver_prev, receiver_now, speed_squared, wavelet,
              source_cell, traces, receiver_cells, plan, stored_snapshots, image_before):
    grid_x, grid_y, depth_cells = source_now.shape
    total_steps = wavelet.shape[0]
    slot_count = plan.shape[0]
    cell_id = source_cell[0]
    site_x = cell_id // (grid_y * depth_cells)
    site_y = (cell_id // depth_cells) % grid_y
    site_z = cell_id % depth_cells
    previous, current = source_prev, source_now
    snapshots = jnp.zeros(stored_snapshots.shape, jnp.bfloat16)
    for step_index in range(total_steps):
        spread = stencil(jnp.pad(current, ((4, 4), (4, 4), (0, 0))))
        spread = spread.at[site_x, site_y, site_z].add(wavelet[step_index])
        latest = 2.0 * current - previous + speed_squared * spread
        previous, current = current, latest
        matches = plan == step_index
        snapshots = jnp.where(matches[:, None, None, None], current.astype(jnp.bfloat16)[None], snapshots)
    source_last, source_final = previous, current

    planes = jnp.zeros((total_steps, grid_x * grid_y), jnp.float32).at[:, receiver_cells[0]].add(traces)
    planes = planes.reshape(total_steps, grid_x, grid_y)
    previous, current = receiver_prev, receiver_now
    imaged = image_before
    for step_index in range(total_steps):
        back_time = total_steps - 1 - step_index
        spread = stencil(jnp.pad(current, ((4, 4), (4, 4), (0, 0))))
        spread = spread.at[:, :, 0].add(planes[back_time])
        latest = 2.0 * current - previous + speed_squared * spread
        previous, current = current, latest
        matches = plan == back_time
        slot_index = jnp.sum(jnp.where(matches, jnp.arange(slot_count, dtype=jnp.int32), 0)).astype(jnp.int32)
        present = jnp.any(matches)
        snapshot = lax.dynamic_index_in_dim(stored_snapshots, slot_index, 0, keepdims=False).astype(jnp.float32)
        imaged = imaged + jnp.where(present, snapshot * current, 0.0)
    return (source_last, source_final, previous, current, snapshots, imaged)
```

```python
import functools
import jax
import jax.numpy as jnp
from jax import lax
from jax.experimental import pallas as pl
from jax.experimental.pallas import tpu as pltpu
from jax.sharding import PartitionSpec as P

STENCIL_COEFFS = (-205.0 / 72.0, 8.0 / 5.0, -1.0 / 5.0, 8.0 / 315.0, -1.0 / 560.0)
LANES = 128
HALF = 4
LOW_X, HIGH_X, LOW_Y, HIGH_Y = range(4)
OPPOSITE = (HIGH_X, LOW_X, HIGH_Y, LOW_Y)
MESH = pl.DeviceIdType.MESH


def kernel(
    total_steps,
    source_prev_hbm,
    source_now_hbm,
    receiver_prev_hbm,
    receiver_now_hbm,
    speed_hbm,
    wavelet_hbm,
    source_cell,
    traces_hbm,
    receiver_cells_hbm,
    hist,
    speed,
    core,
    packed,
    landed,
    records,
    gathered,
    planes,
    inject,
    send_sem,
    recv_sem,
    trace_send,
    trace_recv,
    load_sem,
    source_prev,
    source_now,
    receiver_prev,
    receiver_now,
    speed_squared,
    wavelet,
    traces,
    receiver_cells,
):
    loads = [
        pltpu.make_async_copy(start, end, load_sem.at[i])
        for i, (start, end) in enumerate(
            (
                (source_now_hbm, source_now),
                (receiver_now_hbm, receiver_now),
                (traces_hbm, traces),
                (receiver_cells_hbm, receiver_cells),
                (source_prev_hbm, source_prev),
                (receiver_prev_hbm, receiver_prev),
                (speed_hbm, speed_squared),
                (wavelet_hbm, wavelet),
            )
        )
    ]
    for load in loads:
        load.start()
    block_x, block_y, depth = source_now.shape
    count_x, count_y = lax.axis_size("gx"), lax.axis_size("gy")
    me_x, me_y = lax.axis_index("gx"), lax.axis_index("gy")
    grid_y = block_y * count_y
    peers = count_x * count_y
    me = me_x * count_y + me_y
    tiles = hist.shape[2]
    own = traces.shape[1]
    exists = (me_x > 0, me_x < count_x - 1, me_y > 0, me_y < count_y - 1)
    there = ({"gx": me_x - 1}, {"gx": me_x + 1}, {"gy": me_y - 1}, {"gy": me_y + 1})

    def peer_of(offset):
        other = lax.rem(me + offset, peers)
        return {"gx": other // count_y, "gy": lax.rem(other, count_y)}

    barrier = pltpu.get_barrier_semaphore()

    def greet(offset, carry):
        pl.semaphore_signal(barrier, inc=1, device_id=peer_of(offset), device_id_type=MESH)
        return carry

    lax.fori_loop(1, peers, greet, 0)

    for side in range(4):

        @pl.when(jnp.logical_not(exists[side]))
        def _():
            for field in range(2):
                for parity in range(2):
                    landed[field, parity, side] = jnp.zeros(landed.shape[3:], jnp.float32)

    row = lax.broadcasted_iota(jnp.int32, (block_y, LANES), 0)
    lane = lax.broadcasted_iota(jnp.int32, (block_y, LANES), 1)
    first_half = row < HALF
    spots = lax.rem(row, HALF)

    def only(mask, value):
        return jnp.where(mask, jnp.float32(value), jnp.float32(0.0))

    def turn(tile, shift):
        return pltpu.roll(tile, shift, axis=0) if shift else tile

    inner_y = [None] + [
        only(row >= s, STENCIL_COEFFS[s] if s <= HALF else 0.0)
        + only(row < s, STENCIL_COEFFS[block_y - s] if block_y - s <= HALF else 0.0)
        for s in range(1, block_y)
    ]
    upward = [only(spots < HALF - d, STENCIL_COEFFS[HALF - d]) for d in range(HALF)]
    downward = [only(spots >= d, STENCIL_COEFFS[HALF - d]) for d in range(HALF)]

    def cut(tile_index, array, x):
        low = tile_index * LANES
        size = min(LANES, depth - low)
        return array[x, :, low : low + size], size

    def place(target, array):
        for c in range(tiles):
            for x in range(block_x):
                part, size = cut(c, array, x)
                if size < LANES:
                    target[c, x] = jnp.zeros((block_y, LANES), jnp.float32)
                    target[c, x, :, 0:size] = part
                else:
                    target[c, x] = part

    def halo_copy(field, index, parity, side, into):
        if side == LOW_X:
            face = hist.at[field, index, :, 0:HALF]
        elif side == HIGH_X:
            face = hist.at[field, index, :, block_x - HALF : block_x]
        else:
            face = packed.at[field, side - LOW_Y]
        return pltpu.make_async_remote_copy(
            src_ref=face,
            dst_ref=landed.at[field, parity, into],
            send_sem=send_sem.at[field, side],
            recv_sem=recv_sem.at[field, parity, into],
            device_id=there[side],
            device_id_type=MESH,
        )

    def send(field, index, parity, side):
        @pl.when(exists[side])
        def _():
            halo_copy(field, index, parity, side, OPPOSITE[side]).start()

    def receive(field, index, parity, side):
        @pl.when(exists[side])
        def _():
            halo_copy(field, index, parity, side, side).wait()

    def pack_y(field, index):
        for c in range(tiles):
            for i in range(HALF):
                near, far = hist[field, index, c, i], hist[field, index, c, i + HALF]
                packed[field, 0, c, i] = jnp.where(first_half, near, turn(far, HALF))
                packed[field, 1, c, i] = jnp.where(first_half, turn(near, HALF), far)

    def add_y(field, index, parity):
        for c in range(tiles):
            for i in range(HALF):
                low, high = landed[field, parity, LOW_Y, c, i], landed[field, parity, HIGH_Y, c, i]
                below = upward[0] * low
                above = downward[0] * high
                for d in range(1, HALF):
                    below += upward[d] * turn(low, block_y - d)
                    above += downward[d] * turn(high, d)
                near = jnp.where(first_half, below, turn(above, HALF))
                far = jnp.where(first_half, turn(below, HALF), above)
                hist[field, index, c, i] += speed[c, i] * near
                hist[field, index, c, i + HALF] += speed[c, i + HALF] * far

    def add_x(field, index, parity, side):
        for c in range(tiles):
            faces = [landed[field, parity, side, c, j] for j in range(HALF)]
            for i in range(HALF):
                total = None
                for j in range(HALF):
                    distance = i + HALF - j if side == LOW_X else HALF + j - i
                    if distance <= HALF:
                        term = STENCIL_COEFFS[distance] * faces[j]
                        total = term if total is None else total + term
                x = i if side == LOW_X else block_x - HALF + i
                hist[field, index, c, x] += speed[c, x] * total

    def local(field, index, extra):
        for x in range(block_x):
            centers = [hist[field, index, c, x] for c in range(tiles)]
            spread = []
            for c in range(tiles):
                total = 3.0 * STENCIL_COEFFS[0] * centers[c]
                for s in range(1, block_y):
                    total += inner_y[s] * turn(centers[c], s)
                spread.append(total)
            for k in range(1, HALF + 1):
                forward = [pltpu.roll(center, k, axis=1) for center in centers]
                back = [pltpu.roll(center, LANES - k, axis=1) for center in centers]
                for c in range(tiles):
                    around = jnp.where(lane < k, forward[c - 1] if c else 0.0, forward[c])
                    around += jnp.where(
                        lane < LANES - k, back[c], back[c + 1] if c + 1 < tiles else 0.0
                    )
                    if x >= k:
                        around += hist[field, index, c, x - k]
                    if x + k < block_x:
                        around += hist[field, index, c, x + k]
                    spread[c] += STENCIL_COEFFS[k] * around
            for c in range(tiles):
                latest = 2.0 * centers[c] - hist[field, index - 1, c, x]
                hist[field, index + 1, c, x] = extra(c, x, latest + speed[c, x] * spread[c])

    for load in loads[:4]:
        load.wait()
    place(hist.at[0, 1], source_now)
    place(hist.at[1, 1], receiver_now)
    pack_y(0, 1)
    pack_y(1, 1)
    records[...] = jnp.zeros_like(records)
    records[0:total_steps, 0:own] = traces[...]
    records[total_steps : total_steps + 1, 0:own] = receiver_cells[...].astype(jnp.float32)
    pl.semaphore_wait(barrier, peers - 1)

    def trace_copy(offset):
        return pltpu.make_async_remote_copy(
            src_ref=records,
            dst_ref=gathered.at[offset - 1],
            send_sem=trace_send,
            recv_sem=trace_recv,
            device_id=peer_of(offset),
            device_id_type=MESH,
        )

    def spread_records(offset, carry):
        trace_copy(offset).start()
        return carry

    lax.fori_loop(1, peers, spread_records, 0)
    for field in range(2):
        for side in range(4):
            send(field, 1, 0, side)
    for load in loads[4:]:
        load.wait()
    place(hist.at[0, 0], source_prev)
    place(hist.at[1, 0], receiver_prev)
    place(speed, speed_squared)
    origin = jnp.broadcast_to(source_cell[...].reshape(1, 1), (block_y, LANES))
    for c in range(tiles):
        for x in range(block_x):
            flat = ((me_x * block_x + x) * grid_y + me_y * block_y + row) * depth + c * LANES + lane
            hit = flat == origin
            if (c + 1) * LANES > depth:
                hit &= lane < depth - c * LANES
            core[c, x] = jnp.where(hit, speed[c, x], 0.0)

    def source_extra(step):
        return lambda c, x, latest: latest + wavelet[step] * core[c, x]

    def receiver_extra(step):
        back = total_steps - 1 - step
        return lambda c, x, latest: latest if c else latest + inject[back, x]

    local(0, 1, source_extra(0))
    local(1, 1, lambda c, x, latest: latest)

    def injected(step, x):
        rows = planes[x * block_y : (x + 1) * block_y, :]
        turned = pltpu.roll(rows, LANES - step, axis=1) if step else rows
        return jnp.where(lane == 0, turned * speed[0, x], 0.0)

    def collect_planes():
        everything = pltpu.make_async_remote_copy(
            src_ref=gathered.at[pl.ds(0, peers - 1)],
            dst_ref=gathered.at[pl.ds(0, peers - 1)],
            send_sem=trace_send,
            recv_sem=trace_recv,
            device_id=there[0],
            device_id_type=MESH,
        )
        everything.wait()
        gathered[peers - 1] = records[...]
        cells = block_x * block_y
        number = lax.broadcasted_iota(jnp.int32, (cells, LANES), 0)
        number = (me_x * block_x + number // block_y) * grid_y + me_y * block_y + number % block_y
        number = number.astype(jnp.float32)
        share = LANES // own
        count = records.shape[0]

        def one(first):
            block = gathered[first]
            for j in range(1, share):
                block = block + pltpu.roll(gathered[first + j], j * own, axis=1)
            cell = block[total_steps : total_steps + 1, :]
            chosen = jnp.where(cell == number, jnp.float32(1.0), jnp.float32(0.0))
            high = block.astype(jnp.bfloat16)
            rest = block - high.astype(jnp.float32)
            middle = rest.astype(jnp.bfloat16)
            low = (rest - middle.astype(jnp.float32)).astype(jnp.bfloat16)
            return chosen.astype(jnp.bfloat16), jnp.concatenate([high, middle, low], axis=0)

        group = 16 if peers % 16 == 0 else share

        def several(index, total):
            parts = [one(index * group + j) for j in range(0, group, share)]
            return total + lax.dot_general(
                jnp.concatenate([part[0] for part in parts], axis=1),
                jnp.concatenate([part[1] for part in parts], axis=1),
                (((1,), (1,)), ((), ())),
                preferred_element_type=jnp.float32,
            )

        zero = jnp.zeros((cells, 3 * count), jnp.float32)
        total = several(0, zero) if peers == group else lax.fori_loop(0, peers // group, several, zero)
        planes[...] = jnp.zeros_like(planes)
        planes[:, 0 : 3 * count] = total
        whole = planes[...]
        planes[...] = (
            whole
            + pltpu.roll(whole, LANES - count, axis=1)
            + pltpu.roll(whole, LANES - 2 * count, axis=1)
        )

    def halos(field, step, parity, going):
        index = step + 2
        for side in (LOW_Y, HIGH_Y):
            receive(field, index, parity, side)
        add_y(field, index, parity)
        for side in (LOW_X, HIGH_X):
            receive(field, index, parity, side)
            add_x(field, index, parity, side)
            if going:
                send(field, index, 1 - parity, side)
        if going:
            pack_y(field, index)
            for side in (LOW_Y, HIGH_Y):
                send(field, index, 1 - parity, side)

    halos(0, 0, 0, total_steps > 1)
    if total_steps > 1:
        local(0, 2, source_extra(1))
    collect_planes()
    for x in range(block_x):
        hist[1, 2, 0, x] += injected(total_steps - 1, x)
    halos(1, 0, 0, total_steps > 1)
    for step in range(total_steps - 1):
        for x in range(block_x):
            inject[step, x] = injected(step, x)
    if total_steps > 1:
        local(1, 2, receiver_extra(1))

    def both(step, carry):
        parity = lax.rem(step, 2)
        for field, extra in enumerate((source_extra, receiver_extra)):
            halos(field, step, parity, True)
            local(field, step + 2, extra(step + 1))
        return carry

    lax.fori_loop(1, total_steps - 1, both, 0)
    if total_steps > 1:
        for field in range(2):
            halos(field, total_steps - 1, (total_steps - 1) % 2, False)


def finish(
    total_steps,
    hist,
    plan,
    stored,
    image_before,
    out_source_prev,
    out_source_now,
    out_receiver_prev,
    out_receiver_now,
    out_snapshots,
    out_image,
):
    block_x, block_y, depth = image_before.shape
    for c in range(hist.shape[2]):
        low = c * LANES
        size = min(LANES, depth - low)
        span = slice(low, low + size)
        out_source_prev[:, :, span] = hist[0, total_steps, c, :, :, 0:size]
        out_source_now[:, :, span] = hist[0, total_steps + 1, c, :, :, 0:size]
        out_receiver_prev[:, :, span] = hist[1, total_steps, c, :, :, 0:size]
        out_receiver_now[:, :, span] = hist[1, total_steps + 1, c, :, :, 0:size]
        total = image_before[:, :, span]
        for slot in range(plan.shape[0]):
            taken = hist[0, plan[slot] + 2, c, :, :, 0:size]
            out_snapshots[slot, :, :, span] = taken.astype(jnp.bfloat16)
            taken = hist[1, total_steps + 1 - plan[slot], c, :, :, 0:size]
            total = total + stored[slot, :, :, span].astype(jnp.float32) * taken
        out_image[:, :, span] = total


def body(*arrays):
    source_now, wavelet, traces, stored, plan = (arrays[i] for i in (1, 5, 7, 10, 9))
    block_x, block_y, depth = source_now.shape
    total_steps = wavelet.shape[0]
    peers = lax.axis_size("gx") * lax.axis_size("gy")
    tiles = -(-depth // LANES)
    record_rows = -(-(total_steps + 1) // 8) * 8
    vmem = pl.BlockSpec(memory_space=pltpu.VMEM)
    hbm = pl.BlockSpec(memory_space=pltpu.HBM)
    smem = pl.BlockSpec(memory_space=pltpu.SMEM)
    field = jax.ShapeDtypeStruct(source_now.shape, jnp.float32)
    f32 = jnp.float32
    shape = (2, total_steps + 2, tiles, block_x, block_y, LANES)
    face = (tiles, HALF, block_y, LANES)
    hist = pl.pallas_call(
        functools.partial(kernel, total_steps),
        out_shape=pltpu.VMEM(shape, f32),
        in_specs=[hbm] * 6 + [vmem] + [hbm] * 2,
        out_specs=vmem,
        scratch_shapes=[
            pltpu.VMEM(shape[2:], f32),
            pltpu.VMEM(shape[2:], f32),
            pltpu.VMEM((2, 2) + face, f32),
            pltpu.VMEM((2, 2, 4) + face, f32),
            pltpu.VMEM((record_rows, LANES), f32),
            pltpu.VMEM((peers, record_rows, LANES), f32),
            pltpu.VMEM((block_x * block_y, LANES), f32),
            pltpu.VMEM((total_steps, block_x, block_y, LANES), f32),
            pltpu.SemaphoreType.DMA((2, 4)),
            pltpu.SemaphoreType.DMA((2, 2, 4)),
            pltpu.SemaphoreType.DMA,
            pltpu.SemaphoreType.DMA,
            pltpu.SemaphoreType.DMA((8,)),
            *[pltpu.VMEM(source_now.shape, f32)] * 5,
            pltpu.SMEM(wavelet.shape, f32),
            pltpu.VMEM(traces.shape, f32),
            pltpu.VMEM(arrays[8].shape, jnp.int32),
        ],
        compiler_params=pltpu.CompilerParams(
            collective_id=0, has_side_effects=True, vmem_limit_bytes=24 << 20
        ),
    )(
        *[
            array if i == 6 else pltpu.with_memory_space_constraint(array, pltpu.HBM)
            for i, array in enumerate(arrays[:9])
        ]
    )
    return pl.pallas_call(
        functools.partial(finish, total_steps),
        out_shape=(
            field,
            field,
            field,
            field,
            jax.ShapeDtypeStruct(stored.shape, jnp.bfloat16),
            field,
        ),
        in_specs=[vmem, smem, vmem, vmem],
        out_specs=[vmem] * 6,
        compiler_params=pltpu.CompilerParams(vmem_limit_bytes=24 << 20),
    )(hist, plan, stored, arrays[11])


def solution(mesh):
    block = P(("shot", "gx"), "gy", None)
    kept = P("shot", "gx", "gy", None)
    return jax.shard_map(
        body,
        mesh=mesh,
        in_specs=(
            block,
            block,
            block,
            block,
            block,
            P("shot"),
            P("shot"),
            P("shot", ("gx", "gy")),
            P("shot", ("gx", "gy")),
            P("shot"),
            kept,
            block,
        ),
        out_specs=(block, block, block, block, kept, block),
        check_vma=False,
    )
```

```python
import functools
import jax
import jax.numpy as jnp
from jax import lax
from jax.experimental import pallas as pl
from jax.experimental.pallas import tpu as pltpu
from jax.sharding import PartitionSpec as P

STENCIL_COEFFS = (-205.0 / 72.0, 8.0 / 5.0, -1.0 / 5.0, 8.0 / 315.0, -1.0 / 560.0)
LANES = 128
HALF = 4
LOW_X, HIGH_X, LOW_Y, HIGH_Y = range(4)
OPPOSITE = (HIGH_X, LOW_X, HIGH_Y, LOW_Y)
MESH = pl.DeviceIdType.MESH


def kernel(
    total_steps,
    source_prev_hbm,
    source_now_hbm,
    receiver_prev_hbm,
    receiver_now_hbm,
    speed_hbm,
    wavelet_hbm,
    source_cell,
    traces_hbm,
    receiver_cells_hbm,
    hist,
    speed,
    core,
    packed,
    landed,
    line,
    gathered,
    planes,
    inject,
    send_sem,
    recv_sem,
    line_send,
    line_recv,
    trace_send,
    trace_recv,
    known,
    load_sem,
    source_prev,
    source_now,
    receiver_prev,
    receiver_now,
    speed_squared,
    wavelet,
    traces,
    receiver_cells,
):
    loads = [
        pltpu.make_async_copy(start, end, load_sem.at[i])
        for i, (start, end) in enumerate(
            (
                (source_now_hbm, source_now),
                (receiver_now_hbm, receiver_now),
                (traces_hbm, traces),
                (receiver_cells_hbm, receiver_cells),
                (source_prev_hbm, source_prev),
                (receiver_prev_hbm, receiver_prev),
                (speed_hbm, speed_squared),
                (wavelet_hbm, wavelet),
            )
        )
    ]
    for load in loads:
        load.start()
    block_x, block_y, depth = source_now.shape
    count_x, count_y = lax.axis_size("gx"), lax.axis_size("gy")
    me_x, me_y = lax.axis_index("gx"), lax.axis_index("gy")
    grid_y = block_y * count_y
    tiles = hist.shape[2]
    own = traces.shape[1]
    exists = (me_x > 0, me_x < count_x - 1, me_y > 0, me_y < count_y - 1)
    there = ({"gx": me_x - 1}, {"gx": me_x + 1}, {"gy": me_y - 1}, {"gy": me_y + 1})

    def on_line(offset):
        return {"gy": lax.rem(me_y + offset, count_y)}

    def across(offset):
        return {"gx": lax.rem(me_x + offset, count_x)}

    barrier = pltpu.get_barrier_semaphore()

    def greet(offset, carry):
        pl.semaphore_signal(barrier, inc=1, device_id=on_line(offset), device_id_type=MESH)
        return carry

    for side in (LOW_X, HIGH_X):

        @pl.when(exists[side])
        def _():
            pl.semaphore_signal(barrier, inc=1, device_id=there[side], device_id_type=MESH)

    lax.fori_loop(1, count_y, greet, 0)

    for side in range(4):

        @pl.when(jnp.logical_not(exists[side]))
        def _():
            for field in range(2):
                for parity in range(2):
                    landed[field, parity, side] = jnp.zeros(landed.shape[3:], jnp.float32)

    row = lax.broadcasted_iota(jnp.int32, (block_y, LANES), 0)
    lane = lax.broadcasted_iota(jnp.int32, (block_y, LANES), 1)
    first_half = row < HALF
    spots = lax.rem(row, HALF)

    def only(mask, value):
        return jnp.where(mask, jnp.float32(value), jnp.float32(0.0))

    def turn(tile, shift):
        return pltpu.roll(tile, shift, axis=0) if shift else tile

    inner_y = [None] + [
        only(row >= s, STENCIL_COEFFS[s] if s <= HALF else 0.0)
        + only(row < s, STENCIL_COEFFS[block_y - s] if block_y - s <= HALF else 0.0)
        for s in range(1, block_y)
    ]
    upward = [only(spots < HALF - d, STENCIL_COEFFS[HALF - d]) for d in range(HALF)]
    downward = [only(spots >= d, STENCIL_COEFFS[HALF - d]) for d in range(HALF)]

    def cut(tile_index, array, x):
        low = tile_index * LANES
        size = min(LANES, depth - low)
        return array[x, :, low : low + size], size

    def place(target, array):
        for c in range(tiles):
            for x in range(block_x):
                part, size = cut(c, array, x)
                if size < LANES:
                    target[c, x] = jnp.zeros((block_y, LANES), jnp.float32)
                    target[c, x, :, 0:size] = part
                else:
                    target[c, x] = part

    def halo_copy(field, index, parity, side, c, into):
        if side == LOW_X:
            face = hist.at[field, index, c, 0:HALF]
        elif side == HIGH_X:
            face = hist.at[field, index, c, block_x - HALF : block_x]
        else:
            face = packed.at[field, side - LOW_Y, c]
        return pltpu.make_async_remote_copy(
            src_ref=face,
            dst_ref=landed.at[field, parity, into, c],
            send_sem=send_sem.at[field, side, c],
            recv_sem=recv_sem.at[field, parity, into, c],
            device_id=there[side],
            device_id_type=MESH,
        )

    def send(field, index, parity, side, c):
        @pl.when(exists[side])
        def _():
            halo_copy(field, index, parity, side, c, OPPOSITE[side]).start()

    def receive(field, index, parity, side, c):
        @pl.when(exists[side])
        def _():
            halo_copy(field, index, parity, side, c, side).wait()

    def pack_y(field, index, c):
        for i in range(HALF):
            near, far = hist[field, index, c, i], hist[field, index, c, i + HALF]
            packed[field, 0, c, i] = jnp.where(first_half, near, turn(far, HALF))
            packed[field, 1, c, i] = jnp.where(first_half, turn(near, HALF), far)

    def add_y(field, index, parity, c):
        for i in range(HALF):
            low, high = landed[field, parity, LOW_Y, c, i], landed[field, parity, HIGH_Y, c, i]
            below = upward[0] * low
            above = downward[0] * high
            for d in range(1, HALF):
                below += upward[d] * turn(low, block_y - d)
                above += downward[d] * turn(high, d)
            near = jnp.where(first_half, below, turn(above, HALF))
            far = jnp.where(first_half, turn(below, HALF), above)
            hist[field, index, c, i] += speed[c, i] * near
            hist[field, index, c, i + HALF] += speed[c, i + HALF] * far

    def add_x(field, index, parity, side, c):
        faces = [landed[field, parity, side, c, j] for j in range(HALF)]
        for i in range(HALF):
            total = None
            for j in range(HALF):
                distance = i + HALF - j if side == LOW_X else HALF + j - i
                if distance <= HALF:
                    term = STENCIL_COEFFS[distance] * faces[j]
                    total = term if total is None else total + term
            x = i if side == LOW_X else block_x - HALF + i
            hist[field, index, c, x] += speed[c, x] * total

    def local(field, index, extra):
        for x in range(block_x):
            centers = [hist[field, index, c, x] for c in range(tiles)]
            spread = []
            for c in range(tiles):
                total = 3.0 * STENCIL_COEFFS[0] * centers[c]
                for s in range(1, block_y):
                    total += inner_y[s] * turn(centers[c], s)
                spread.append(total)
            for k in range(1, HALF + 1):
                forward = [pltpu.roll(center, k, axis=1) for center in centers]
                back = [pltpu.roll(center, LANES - k, axis=1) for center in centers]
                for c in range(tiles):
                    around = jnp.where(lane < k, forward[c - 1] if c else 0.0, forward[c])
                    around += jnp.where(
                        lane < LANES - k, back[c], back[c + 1] if c + 1 < tiles else 0.0
                    )
                    if x >= k:
                        around += hist[field, index, c, x - k]
                    if x + k < block_x:
                        around += hist[field, index, c, x + k]
                    spread[c] += STENCIL_COEFFS[k] * around
            for c in range(tiles):
                latest = 2.0 * centers[c] - hist[field, index - 1, c, x]
                hist[field, index + 1, c, x] = extra(c, x, latest + speed[c, x] * spread[c])

    for load in loads[:4]:
        load.wait()
    place(hist.at[0, 1], source_now)
    place(hist.at[1, 1], receiver_now)
    for field in range(2):
        for c in range(tiles):
            pack_y(field, 1, c)
    rows = -(-total_steps // 2)
    mine = line.at[me_y]
    mine[...] = jnp.zeros((block_y, LANES), jnp.float32)
    mine[0:rows, 0:own] = traces[0:rows, :]
    mine[0 : total_steps - rows, own : 2 * own] = traces[rows:total_steps, :]
    mine[rows : rows + 1, 0:own] = receiver_cells[...].astype(jnp.float32)
    mine[rows : rows + 1, own : 2 * own] = receiver_cells[...].astype(jnp.float32)
    beside = [exists[side].astype(jnp.int32) for side in (LOW_X, HIGH_X)]
    pl.semaphore_wait(barrier, count_y - 1 + beside[0] + beside[1])

    def line_copy(offset):
        return pltpu.make_async_remote_copy(
            src_ref=line.at[me_y],
            dst_ref=line.at[me_y],
            send_sem=line_send,
            recv_sem=line_recv,
            device_id=on_line(offset),
            device_id_type=MESH,
        )

    def spread_line(offset, carry):
        line_copy(offset).start()
        return carry

    def tell(turn_number):
        for side in (LOW_X, HIGH_X):

            @pl.when(exists[side])
            def _():
                pl.semaphore_signal(
                    known.at[turn_number, OPPOSITE[side]],
                    inc=1,
                    device_id=there[side],
                    device_id_type=MESH,
                )

    def hear(turn_number):
        for side in (LOW_X, HIGH_X):

            @pl.when(exists[side])
            def _():
                pl.semaphore_wait(known.at[turn_number, side], 1)

    def pass_on(turn_number, carry):
        hear(turn_number - 1)
        tell(turn_number)
        return carry

    rounds = count_x - 2
    lax.fori_loop(1, count_y, spread_line, 0)
    if rounds > 0:
        tell(0)
    for c in range(tiles):
        for field in range(2):
            for side in range(4):
                send(field, 1, 0, side, c)
    for load in loads[4:]:
        load.wait()
    place(hist.at[0, 0], source_prev)
    place(speed, speed_squared)
    origin = jnp.broadcast_to(source_cell[...].reshape(1, 1), (block_y, LANES))
    for c in range(tiles):
        for x in range(block_x):
            flat = ((me_x * block_x + x) * grid_y + me_y * block_y + row) * depth + c * LANES + lane
            hit = flat == origin
            if (c + 1) * LANES > depth:
                hit &= lane < depth - c * LANES
            core[c, x] = jnp.where(hit, speed[c, x], 0.0)

    def source_extra(step):
        return lambda c, x, latest: latest + wavelet[step] * core[c, x]

    def receiver_extra(step):
        back = total_steps - 1 - step
        return lambda c, x, latest: latest if c else latest + inject[back, x]

    if rounds > 1:
        lax.fori_loop(1, rounds, pass_on, 0)
    local(0, 1, source_extra(0))
    if rounds > 0:
        hear(rounds - 1)

    def trace_copy(offset):
        return pltpu.make_async_remote_copy(
            src_ref=line,
            dst_ref=gathered.at[me_x],
            send_sem=trace_send,
            recv_sem=trace_recv,
            device_id=across(offset),
            device_id_type=MESH,
        )

    def spread_traces(offset, carry):
        trace_copy(offset).start()
        return carry

    everyone = pltpu.make_async_remote_copy(
        src_ref=line.at[pl.ds(0, count_y - 1)],
        dst_ref=line.at[pl.ds(0, count_y - 1)],
        send_sem=line_send,
        recv_sem=line_recv,
        device_id=on_line(1),
        device_id_type=MESH,
    )
    everyone.wait()
    lax.fori_loop(1, count_x, spread_traces, 0)
    gathered[me_x] = line[...]
    place(hist.at[1, 0], receiver_prev)
    local(1, 1, lambda c, x, latest: latest)

    def injected(step, x):
        values = planes[x * block_y : (x + 1) * block_y, :]
        spot = step if step < rows else block_y + step - rows
        turned = pltpu.roll(values, LANES - spot, axis=1) if spot else values
        return jnp.where(lane == 0, turned * speed[0, x], 0.0)

    def collect_planes():
        everything = pltpu.make_async_remote_copy(
            src_ref=gathered.at[pl.ds(0, count_x - 1)],
            dst_ref=gathered.at[pl.ds(0, count_x - 1)],
            send_sem=trace_send,
            recv_sem=trace_recv,
            device_id=across(1),
            device_id_type=MESH,
        )
        everything.wait()
        cells = block_x * block_y
        number = lax.broadcasted_iota(jnp.int32, (cells, LANES), 0)
        number = (me_x * block_x + number // block_y) * grid_y + me_y * block_y + number % block_y
        number = number.astype(jnp.float32)

        def one(x, y):
            block = gathered[x, y]
            chosen = jnp.where(block[rows : rows + 1, :] == number, jnp.float32(1.0), jnp.float32(0.0))
            both = jnp.concatenate(
                [jnp.where(lane < own, block, 0.0), jnp.where(lane < own, 0.0, block)], axis=0
            )
            high = both.astype(jnp.bfloat16)
            rest = both - high.astype(jnp.float32)
            middle = rest.astype(jnp.bfloat16)
            low = (rest - middle.astype(jnp.float32)).astype(jnp.bfloat16)
            return chosen.astype(jnp.bfloat16), jnp.concatenate([high, middle, low], axis=0)

        count = 2 * block_y
        near = min(count_y, 4)

        def several(index, total):
            x, y = index // (count_y // near), lax.rem(index, count_y // near) * near
            parts = [one(x, y + j) for j in range(near)]
            return total + lax.dot_general(
                jnp.concatenate([part[0] for part in parts], axis=1),
                jnp.concatenate([part[1] for part in parts], axis=1),
                (((1,), (1,)), ((), ())),
                preferred_element_type=jnp.float32,
            )

        total = jnp.zeros((cells, 3 * count), jnp.float32)
        groups = count_x * count_y // near
        if groups <= 4:
            for index in range(groups):
                total = several(index, total)
        else:
            total = lax.fori_loop(0, groups, several, total)
        planes[...] = jnp.zeros_like(planes)
        planes[:, 0 : 3 * count] = total
        whole = planes[...]
        planes[...] = (
            whole
            + pltpu.roll(whole, LANES - count, axis=1)
            + pltpu.roll(whole, LANES - 2 * count, axis=1)
        )

    def halos(field, step, parity, going):
        index = step + 2
        for c in range(tiles):
            for side in (LOW_Y, HIGH_Y):
                receive(field, index, parity, side, c)
            add_y(field, index, parity, c)
            for side in (LOW_X, HIGH_X):
                receive(field, index, parity, side, c)
            for side in (LOW_X, HIGH_X):
                add_x(field, index, parity, side, c)
            if going:
                for side in (LOW_X, HIGH_X):
                    send(field, index, 1 - parity, side, c)
                pack_y(field, index, c)
                for side in (LOW_Y, HIGH_Y):
                    send(field, index, 1 - parity, side, c)

    halos(0, 0, 0, total_steps > 1)
    if total_steps > 1:
        local(0, 2, source_extra(1))
    collect_planes()
    for x in range(block_x):
        hist[1, 2, 0, x] += injected(total_steps - 1, x)
    halos(1, 0, 0, total_steps > 1)
    for step in range(total_steps - 1):
        for x in range(block_x):
            inject[step, x] = injected(step, x)
    if total_steps > 1:
        local(1, 2, receiver_extra(1))

    def both(step, carry):
        parity = lax.rem(step, 2)
        for field, extra in enumerate((source_extra, receiver_extra)):
            halos(field, step, parity, True)
            local(field, step + 2, extra(step + 1))
        return carry

    lax.fori_loop(1, total_steps - 1, both, 0)
    if total_steps > 1:
        for field in range(2):
            halos(field, total_steps - 1, (total_steps - 1) % 2, False)


def finish(
    total_steps,
    hist,
    plan,
    stored,
    image_before,
    out_source_prev,
    out_source_now,
    out_receiver_prev,
    out_receiver_now,
    out_snapshots,
    out_image,
):
    block_x, block_y, depth = image_before.shape
    for c in range(hist.shape[2]):
        low = c * LANES
        size = min(LANES, depth - low)
        span = slice(low, low + size)
        out_source_prev[:, :, span] = hist[0, total_steps, c, :, :, 0:size]
        out_source_now[:, :, span] = hist[0, total_steps + 1, c, :, :, 0:size]
        out_receiver_prev[:, :, span] = hist[1, total_steps, c, :, :, 0:size]
        out_receiver_now[:, :, span] = hist[1, total_steps + 1, c, :, :, 0:size]
        total = image_before[:, :, span]
        for slot in range(plan.shape[0]):
            taken = hist[0, plan[slot] + 2, c, :, :, 0:size]
            out_snapshots[slot, :, :, span] = taken.astype(jnp.bfloat16)
            taken = hist[1, total_steps + 1 - plan[slot], c, :, :, 0:size]
            total = total + stored[slot, :, :, span].astype(jnp.float32) * taken
        out_image[:, :, span] = total


def body(*arrays):
    source_now, wavelet, traces, stored, plan = (arrays[i] for i in (1, 5, 7, 10, 9))
    block_x, block_y, depth = source_now.shape
    total_steps = wavelet.shape[0]
    count_x, count_y = lax.axis_size("gx"), lax.axis_size("gy")
    tiles = -(-depth // LANES)
    vmem = pl.BlockSpec(memory_space=pltpu.VMEM)
    hbm = pl.BlockSpec(memory_space=pltpu.HBM)
    smem = pl.BlockSpec(memory_space=pltpu.SMEM)
    field = jax.ShapeDtypeStruct(source_now.shape, jnp.float32)
    f32 = jnp.float32
    shape = (2, total_steps + 2, tiles, block_x, block_y, LANES)
    face = (tiles, HALF, block_y, LANES)
    hist = pl.pallas_call(
        functools.partial(kernel, total_steps),
        out_shape=pltpu.VMEM(shape, f32),
        in_specs=[hbm] * 6 + [vmem] + [hbm] * 2,
        out_specs=vmem,
        scratch_shapes=[
            pltpu.VMEM(shape[2:], f32),
            pltpu.VMEM(shape[2:], f32),
            pltpu.VMEM((2, 2) + face, f32),
            pltpu.VMEM((2, 2, 4) + face, f32),
            pltpu.VMEM((count_y, block_y, LANES), f32),
            pltpu.VMEM((count_x, count_y, block_y, LANES), f32),
            pltpu.VMEM((block_x * block_y, LANES), f32),
            pltpu.VMEM((total_steps, block_x, block_y, LANES), f32),
            pltpu.SemaphoreType.DMA((2, 4, tiles)),
            pltpu.SemaphoreType.DMA((2, 2, 4, tiles)),
            pltpu.SemaphoreType.DMA,
            pltpu.SemaphoreType.DMA,
            pltpu.SemaphoreType.DMA,
            pltpu.SemaphoreType.DMA,
            pltpu.SemaphoreType.REGULAR((max(count_x - 2, 1), 2)),
            pltpu.SemaphoreType.DMA((8,)),
            *[pltpu.VMEM(source_now.shape, f32)] * 5,
            pltpu.SMEM(wavelet.shape, f32),
            pltpu.VMEM(traces.shape, f32),
            pltpu.VMEM(arrays[8].shape, jnp.int32),
        ],
        compiler_params=pltpu.CompilerParams(
            collective_id=0, has_side_effects=True, vmem_limit_bytes=24 << 20
        ),
    )(
        *[
            array if i == 6 else pltpu.with_memory_space_constraint(array, pltpu.HBM)
            for i, array in enumerate(arrays[:9])
        ]
    )
    return pl.pallas_call(
        functools.partial(finish, total_steps),
        out_shape=(
            field,
            field,
            field,
            field,
            jax.ShapeDtypeStruct(stored.shape, jnp.bfloat16),
            field,
        ),
        in_specs=[vmem, smem, vmem, vmem],
        out_specs=[vmem] * 6,
        compiler_params=pltpu.CompilerParams(vmem_limit_bytes=24 << 20),
    )(hist, plan, stored, arrays[11])


def solution(mesh):
    block = P(("shot", "gx"), "gy", None)
    kept = P("shot", "gx", "gy", None)
    return jax.shard_map(
        body,
        mesh=mesh,
        in_specs=(
            block,
            block,
            block,
            block,
            block,
            P("shot"),
            P("shot"),
            P("shot", ("gx", "gy")),
            P("shot", ("gx", "gy")),
            P("shot"),
            kept,
            block,
        ),
        out_specs=(block, block, block, block, kept, block),
        check_vma=False,
    )
```

```python
import functools
import jax
import jax.numpy as jnp
from jax import lax
from jax.experimental import pallas as pl
from jax.experimental.pallas import tpu as pltpu
from jax.sharding import PartitionSpec as P

STENCIL_COEFFS = (-205.0 / 72.0, 8.0 / 5.0, -1.0 / 5.0, 8.0 / 315.0, -1.0 / 560.0)
LANES = 128
HALF = 4
LOW_X, HIGH_X, LOW_Y, HIGH_Y = range(4)
OPPOSITE = (HIGH_X, LOW_X, HIGH_Y, LOW_Y)
MESH = pl.DeviceIdType.MESH


def kernel(
    total_steps,
    source_prev_hbm,
    source_now_hbm,
    receiver_prev_hbm,
    receiver_now_hbm,
    speed_hbm,
    wavelet_hbm,
    source_cell,
    traces_hbm,
    receiver_cells_hbm,
    hist,
    speed,
    core,
    packed,
    landed,
    speed_packed,
    speed_landed,
    line,
    gathered,
    planes,
    inject,
    send_sem,
    recv_sem,
    line_send,
    line_recv,
    trace_send,
    trace_recv,
    known,
    speed_send,
    speed_recv,
    load_sem,
    source_prev,
    source_now,
    receiver_prev,
    receiver_now,
    speed_squared,
    wavelet,
    traces,
    receiver_cells,
):
    loads = [
        pltpu.make_async_copy(start, end, load_sem.at[i])
        for i, (start, end) in enumerate(
            (
                (source_now_hbm, source_now),
                (receiver_now_hbm, receiver_now),
                (traces_hbm, traces),
                (receiver_cells_hbm, receiver_cells),
                (source_prev_hbm, source_prev),
                (receiver_prev_hbm, receiver_prev),
                (speed_hbm, speed_squared),
                (wavelet_hbm, wavelet),
            )
        )
    ]
    for load in loads:
        load.start()
    block_x, block_y, depth = source_now.shape
    count_x, count_y = lax.axis_size("gx"), lax.axis_size("gy")
    me_x, me_y = lax.axis_index("gx"), lax.axis_index("gy")
    grid_y = block_y * count_y
    tiles = hist.shape[2]
    own = traces.shape[1]
    exists = (me_x > 0, me_x < count_x - 1, me_y > 0, me_y < count_y - 1)
    there = ({"gx": me_x - 1}, {"gx": me_x + 1}, {"gy": me_y - 1}, {"gy": me_y + 1})

    def on_line(offset):
        return {"gy": lax.rem(me_y + offset, count_y)}

    def across(offset):
        return {"gx": lax.rem(me_x + offset, count_x)}

    barrier = pltpu.get_barrier_semaphore()

    def greet(offset, carry):
        pl.semaphore_signal(barrier, inc=1, device_id=on_line(offset), device_id_type=MESH)
        return carry

    for side in (LOW_X, HIGH_X):

        @pl.when(exists[side])
        def _():
            pl.semaphore_signal(barrier, inc=1, device_id=there[side], device_id_type=MESH)

    lax.fori_loop(1, count_y, greet, 0)

    for side in range(4):

        @pl.when(jnp.logical_not(exists[side]))
        def _():
            for field in range(2):
                for parity in range(2):
                    landed[field, parity, side] = jnp.zeros(landed.shape[3:], jnp.float32)
            speed_landed[side] = jnp.zeros(speed_landed.shape[1:], jnp.float32)

    row = lax.broadcasted_iota(jnp.int32, (block_y, LANES), 0)
    lane = lax.broadcasted_iota(jnp.int32, (block_y, LANES), 1)
    first_half = row < HALF
    spots = lax.rem(row, HALF)

    def only(mask, value):
        return jnp.where(mask, jnp.float32(value), jnp.float32(0.0))

    def turn(tile, shift):
        return pltpu.roll(tile, shift, axis=0) if shift else tile

    inner_y = [None] + [
        only(row >= s, STENCIL_COEFFS[s] if s <= HALF else 0.0)
        + only(row < s, STENCIL_COEFFS[block_y - s] if block_y - s <= HALF else 0.0)
        for s in range(1, block_y)
    ]
    upward = [only(spots < HALF - d, STENCIL_COEFFS[HALF - d]) for d in range(HALF)]
    downward = [only(spots >= d, STENCIL_COEFFS[HALF - d]) for d in range(HALF)]

    def cut(tile_index, array, x):
        low = tile_index * LANES
        size = min(LANES, depth - low)
        return array[x, :, low : low + size], size

    def place(target, array):
        for c in range(tiles):
            for x in range(block_x):
                part, size = cut(c, array, x)
                if size < LANES:
                    target[c, x] = jnp.zeros((block_y, LANES), jnp.float32)
                    target[c, x, :, 0:size] = part
                else:
                    target[c, x] = part

    def halo_copy(field, index, parity, side, c, into):
        if side == LOW_X:
            face = hist.at[field, index, c, 0:HALF]
        elif side == HIGH_X:
            face = hist.at[field, index, c, block_x - HALF : block_x]
        else:
            face = packed.at[field, side - LOW_Y, c]
        return pltpu.make_async_remote_copy(
            src_ref=face,
            dst_ref=landed.at[field, parity, into, c],
            send_sem=send_sem.at[field, side, c],
            recv_sem=recv_sem.at[field, parity, into, c],
            device_id=there[side],
            device_id_type=MESH,
        )

    def send(field, index, parity, side, c):
        @pl.when(exists[side])
        def _():
            halo_copy(field, index, parity, side, c, OPPOSITE[side]).start()

    def receive(field, index, parity, side, c, left=False):
        @pl.when(exists[side])
        def _():
            copy = halo_copy(field, index, parity, side, c, side)
            copy.wait_recv() if left else copy.wait()

    def pack_y(field, index, c):
        for i in range(HALF):
            near, far = hist[field, index, c, i], hist[field, index, c, i + HALF]
            packed[field, 0, c, i] = jnp.where(first_half, near, turn(far, HALF))
            packed[field, 1, c, i] = jnp.where(first_half, turn(near, HALF), far)

    def add_y(field, index, parity, c):
        for i in range(HALF):
            low, high = landed[field, parity, LOW_Y, c, i], landed[field, parity, HIGH_Y, c, i]
            below = upward[0] * low
            above = downward[0] * high
            for d in range(1, HALF):
                below += upward[d] * turn(low, block_y - d)
                above += downward[d] * turn(high, d)
            near = jnp.where(first_half, below, turn(above, HALF))
            far = jnp.where(first_half, turn(below, HALF), above)
            hist[field, index, c, i] += speed[c, i] * near
            hist[field, index, c, i + HALF] += speed[c, i + HALF] * far

    def add_x(field, index, parity, side, c):
        faces = [landed[field, parity, side, c, j] for j in range(HALF)]
        for i in range(HALF):
            total = None
            for j in range(HALF):
                distance = i + HALF - j if side == LOW_X else HALF + j - i
                if distance <= HALF:
                    term = STENCIL_COEFFS[distance] * faces[j]
                    total = term if total is None else total + term
            x = i if side == LOW_X else block_x - HALF + i
            hist[field, index, c, x] += speed[c, x] * total

    def local(field, index, extra):
        for x in range(block_x):
            centers = [hist[field, index, c, x] for c in range(tiles)]
            spread = []
            for c in range(tiles):
                total = 3.0 * STENCIL_COEFFS[0] * centers[c]
                for s in range(1, block_y):
                    total += inner_y[s] * turn(centers[c], s)
                spread.append(total)
            for k in range(1, HALF + 1):
                forward = [pltpu.roll(center, k, axis=1) for center in centers]
                back = [pltpu.roll(center, LANES - k, axis=1) for center in centers]
                for c in range(tiles):
                    around = jnp.where(lane < k, forward[c - 1] if c else 0.0, forward[c])
                    around += jnp.where(
                        lane < LANES - k, back[c], back[c + 1] if c + 1 < tiles else 0.0
                    )
                    if x >= k:
                        around += hist[field, index, c, x - k]
                    if x + k < block_x:
                        around += hist[field, index, c, x + k]
                    spread[c] += STENCIL_COEFFS[k] * around
            for c in range(tiles):
                latest = 2.0 * centers[c] - hist[field, index - 1, c, x]
                hist[field, index + 1, c, x] = extra(c, x, latest + speed[c, x] * spread[c])

    for load in loads[:4]:
        load.wait()
    place(hist.at[0, 1], source_now)
    place(hist.at[1, 1], receiver_now)
    for field in range(2):
        for c in range(tiles):
            pack_y(field, 1, c)
    rows = -(-total_steps // 2)
    mine = line.at[me_y]
    mine[...] = jnp.zeros((block_y, LANES), jnp.float32)
    mine[0:rows, 0:own] = traces[0:rows, :]
    mine[0 : total_steps - rows, own : 2 * own] = traces[rows:total_steps, :]
    mine[rows : rows + 1, 0:own] = receiver_cells[...].astype(jnp.float32)
    mine[rows : rows + 1, own : 2 * own] = receiver_cells[...].astype(jnp.float32)
    beside = [exists[side].astype(jnp.int32) for side in (LOW_X, HIGH_X)]
    pl.semaphore_wait(barrier, count_y - 1 + beside[0] + beside[1])

    def line_copy(offset):
        return pltpu.make_async_remote_copy(
            src_ref=line.at[me_y],
            dst_ref=line.at[me_y],
            send_sem=line_send,
            recv_sem=line_recv,
            device_id=on_line(offset),
            device_id_type=MESH,
        )

    def spread_line(offset, carry):
        line_copy(offset).start()
        return carry

    def tell(turn_number):
        for side in (LOW_X, HIGH_X):

            @pl.when(exists[side])
            def _():
                pl.semaphore_signal(
                    known.at[turn_number, OPPOSITE[side]],
                    inc=1,
                    device_id=there[side],
                    device_id_type=MESH,
                )

    def hear(turn_number):
        for side in (LOW_X, HIGH_X):

            @pl.when(exists[side])
            def _():
                pl.semaphore_wait(known.at[turn_number, side], 1)

    def pass_on(turn_number, carry):
        hear(turn_number - 1)
        tell(turn_number)
        return carry

    rounds = count_x - 2
    lax.fori_loop(1, count_y, spread_line, 0)
    if rounds > 0:
        tell(0)
    for c in range(tiles):
        for field in range(2):
            for side in range(4):
                send(field, 1, 0, side, c)
    for load in loads[4:]:
        load.wait()
    place(speed, speed_squared)

    def speed_copy(side, into):
        if side == LOW_X:
            face = speed.at[0, 0:HALF]
        elif side == HIGH_X:
            face = speed.at[0, block_x - HALF : block_x]
        else:
            face = speed_packed.at[side - LOW_Y]
        return pltpu.make_async_remote_copy(
            src_ref=face,
            dst_ref=speed_landed.at[into],
            send_sem=speed_send.at[side],
            recv_sem=speed_recv.at[into],
            device_id=there[side],
            device_id_type=MESH,
        )

    for i in range(HALF):
        near, far = speed[0, i], speed[0, i + HALF]
        speed_packed[0, i] = jnp.where(first_half, near, turn(far, HALF))
        speed_packed[1, i] = jnp.where(first_half, turn(near, HALF), far)
    for side in range(4):

        @pl.when(exists[side])
        def _():
            speed_copy(side, OPPOSITE[side]).start()

    place(hist.at[0, 0], source_prev)
    origin = jnp.broadcast_to(source_cell[...].reshape(1, 1), (block_y, LANES))
    for c in range(tiles):
        for x in range(block_x):
            flat = ((me_x * block_x + x) * grid_y + me_y * block_y + row) * depth + c * LANES + lane
            hit = flat == origin
            if (c + 1) * LANES > depth:
                hit &= lane < depth - c * LANES
            core[c, x] = jnp.where(hit, speed[c, x], 0.0)

    def source_extra(step):
        return lambda c, x, latest: latest + wavelet[step] * core[c, x]

    def receiver_extra(step):
        back = total_steps - 1 - step
        return lambda c, x, latest: latest if c else latest + inject[back, x]

    if rounds > 1:
        lax.fori_loop(1, rounds, pass_on, 0)
    local(0, 1, source_extra(0))
    if rounds > 0:
        hear(rounds - 1)

    def trace_copy(offset):
        return pltpu.make_async_remote_copy(
            src_ref=line,
            dst_ref=gathered.at[me_x],
            send_sem=trace_send,
            recv_sem=trace_recv,
            device_id=across(offset),
            device_id_type=MESH,
        )

    def spread_traces(offset, carry):
        trace_copy(offset).start()
        return carry

    everyone = pltpu.make_async_remote_copy(
        src_ref=line.at[pl.ds(0, count_y - 1)],
        dst_ref=line.at[pl.ds(0, count_y - 1)],
        send_sem=line_send,
        recv_sem=line_recv,
        device_id=on_line(1),
        device_id_type=MESH,
    )
    everyone.wait()
    lax.fori_loop(1, count_x, spread_traces, 0)
    gathered[me_x] = line[...]
    place(hist.at[1, 0], receiver_prev)
    local(1, 1, lambda c, x, latest: latest)

    def injected(step, x, factor):
        values = planes[x * block_y : (x + 1) * block_y, :]
        spot = step if step < rows else block_y + step - rows
        turned = pltpu.roll(values, LANES - spot, axis=1) if spot else values
        return jnp.where(lane == 0, turned * factor, 0.0)

    def collect_planes():
        everything = pltpu.make_async_remote_copy(
            src_ref=gathered.at[pl.ds(0, count_x - 1)],
            dst_ref=gathered.at[pl.ds(0, count_x - 1)],
            send_sem=trace_send,
            recv_sem=trace_recv,
            device_id=across(1),
            device_id_type=MESH,
        )
        everything.wait()
        cells = planes.shape[0]
        origin_x, origin_y = me_x * block_x, me_y * block_y
        sites = [(origin_x + x, origin_y + row) for x in range(block_x)]
        sites += [(origin_x - HALF + i, origin_y + row) for i in range(HALF)]
        sites += [(origin_x + block_x + i, origin_y + row) for i in range(HALF)]
        for edge in (origin_y - HALF, origin_y + block_y):
            sites += [
                (origin_x + i + jnp.where(first_half, 0, HALF), edge + spots) for i in range(HALF)
            ]
        number = jnp.concatenate(
            [(at_x * grid_y + at_y).astype(jnp.float32) for at_x, at_y in sites], axis=0
        )

        def one(x, y):
            block = gathered[x, y]
            chosen = jnp.where(block[rows : rows + 1, :] == number, jnp.float32(1.0), jnp.float32(0.0))
            both = jnp.concatenate(
                [jnp.where(lane < own, block, 0.0), jnp.where(lane < own, 0.0, block)], axis=0
            )
            high = both.astype(jnp.bfloat16)
            rest = both - high.astype(jnp.float32)
            middle = rest.astype(jnp.bfloat16)
            low = (rest - middle.astype(jnp.float32)).astype(jnp.bfloat16)
            return chosen.astype(jnp.bfloat16), jnp.concatenate([high, middle, low], axis=0)

        count = 2 * block_y
        near = min(count_y, 4)

        def several(index, total):
            x, y = index // (count_y // near), lax.rem(index, count_y // near) * near
            parts = [one(x, y + j) for j in range(near)]
            return total + lax.dot_general(
                jnp.concatenate([part[0] for part in parts], axis=1),
                jnp.concatenate([part[1] for part in parts], axis=1),
                (((1,), (1,)), ((), ())),
                preferred_element_type=jnp.float32,
            )

        total = jnp.zeros((cells, 3 * count), jnp.float32)
        groups = count_x * count_y // near
        if groups <= 4:
            for index in range(groups):
                total = several(index, total)
        else:
            total = lax.fori_loop(0, groups, several, total)
        planes[...] = jnp.zeros_like(planes)
        planes[:, 0 : 3 * count] = total
        whole = planes[...]
        planes[...] = (
            whole
            + pltpu.roll(whole, LANES - count, axis=1)
            + pltpu.roll(whole, LANES - 2 * count, axis=1)
        )

    def patch(parity, side):
        @pl.when(exists[side])
        def _():
            speed_copy(side, side).wait()
            for i in range(HALF):
                late = injected(total_steps - 1, block_x + side * HALF + i, speed_landed[side, i])
                landed[1, parity, side, 0, i] += late

    def halos(field, step, parity, going, patched=False):
        index = step + 2
        for c in range(tiles):
            for side in (LOW_Y, HIGH_Y):
                receive(field, index, parity, side, c)
                if patched and c == 0:
                    patch(parity, side)
            add_y(field, index, parity, c)
            for side in (LOW_X, HIGH_X):
                receive(field, index, parity, side, c, patched and c == 0)
                if patched and c == 0:
                    patch(parity, side)
            for side in (LOW_X, HIGH_X):
                add_x(field, index, parity, side, c)
            if going:
                for side in (LOW_X, HIGH_X):
                    send(field, index, 1 - parity, side, c)
                pack_y(field, index, c)
                for side in (LOW_Y, HIGH_Y):
                    send(field, index, 1 - parity, side, c)

    halos(0, 0, 0, True)
    local(0, 2, source_extra(1))
    halos(1, 0, 0, True)
    collect_planes()
    for side in (LOW_X, HIGH_X):

        @pl.when(exists[side])
        def _():
            halo_copy(1, 2, 1, side, 0, side).wait_send()

    for x in range(block_x):
        hist[1, 2, 0, x] += injected(total_steps - 1, x, speed[0, x])
        inject[total_steps - 2, x] = injected(total_steps - 2, x, speed[0, x])
    local(1, 2, receiver_extra(1))
    halos(0, 1, 1, True)
    for step in range(total_steps - 2):
        for x in range(block_x):
            inject[step, x] = injected(step, x, speed[0, x])
    local(0, 3, source_extra(2))
    halos(1, 1, 1, True, True)
    local(1, 3, receiver_extra(2))

    def both(step, carry):
        parity = lax.rem(step, 2)
        for field, extra in enumerate((source_extra, receiver_extra)):
            halos(field, step, parity, True)
            local(field, step + 2, extra(step + 1))
        return carry

    lax.fori_loop(2, total_steps - 1, both, 0)
    for field in range(2):
        halos(field, total_steps - 1, (total_steps - 1) % 2, False)


def finish(
    total_steps,
    hist,
    plan,
    stored,
    image_before,
    out_source_prev,
    out_source_now,
    out_receiver_prev,
    out_receiver_now,
    out_snapshots,
    out_image,
):
    block_x, block_y, depth = image_before.shape
    for c in range(hist.shape[2]):
        low = c * LANES
        size = min(LANES, depth - low)
        span = slice(low, low + size)
        out_source_prev[:, :, span] = hist[0, total_steps, c, :, :, 0:size]
        out_source_now[:, :, span] = hist[0, total_steps + 1, c, :, :, 0:size]
        out_receiver_prev[:, :, span] = hist[1, total_steps, c, :, :, 0:size]
        out_receiver_now[:, :, span] = hist[1, total_steps + 1, c, :, :, 0:size]
        total = image_before[:, :, span]
        for slot in range(plan.shape[0]):
            taken = hist[0, plan[slot] + 2, c, :, :, 0:size]
            out_snapshots[slot, :, :, span] = taken.astype(jnp.bfloat16)
            taken = hist[1, total_steps + 1 - plan[slot], c, :, :, 0:size]
            total = total + stored[slot, :, :, span].astype(jnp.float32) * taken
        out_image[:, :, span] = total


def body(*arrays):
    source_now, wavelet, traces, stored, plan = (arrays[i] for i in (1, 5, 7, 10, 9))
    block_x, block_y, depth = source_now.shape
    total_steps = wavelet.shape[0]
    count_x, count_y = lax.axis_size("gx"), lax.axis_size("gy")
    tiles = -(-depth // LANES)
    vmem = pl.BlockSpec(memory_space=pltpu.VMEM)
    hbm = pl.BlockSpec(memory_space=pltpu.HBM)
    smem = pl.BlockSpec(memory_space=pltpu.SMEM)
    field = jax.ShapeDtypeStruct(source_now.shape, jnp.float32)
    f32 = jnp.float32
    shape = (2, total_steps + 2, tiles, block_x, block_y, LANES)
    face = (tiles, HALF, block_y, LANES)
    hist = pl.pallas_call(
        functools.partial(kernel, total_steps),
        out_shape=pltpu.VMEM(shape, f32),
        in_specs=[hbm] * 6 + [vmem] + [hbm] * 2,
        out_specs=vmem,
        scratch_shapes=[
            pltpu.VMEM(shape[2:], f32),
            pltpu.VMEM(shape[2:], f32),
            pltpu.VMEM((2, 2) + face, f32),
            pltpu.VMEM((2, 2, 4) + face, f32),
            pltpu.VMEM((2,) + face[1:], f32),
            pltpu.VMEM((4,) + face[1:], f32),
            pltpu.VMEM((count_y, block_y, LANES), f32),
            pltpu.VMEM((count_x, count_y, block_y, LANES), f32),
            pltpu.VMEM(((block_x + 4 * HALF) * block_y, LANES), f32),
            pltpu.VMEM((total_steps, block_x, block_y, LANES), f32),
            pltpu.SemaphoreType.DMA((2, 4, tiles)),
            pltpu.SemaphoreType.DMA((2, 2, 4, tiles)),
            pltpu.SemaphoreType.DMA,
            pltpu.SemaphoreType.DMA,
            pltpu.SemaphoreType.DMA,
            pltpu.SemaphoreType.DMA,
            pltpu.SemaphoreType.REGULAR((max(count_x - 2, 1), 2)),
            pltpu.SemaphoreType.DMA((4,)),
            pltpu.SemaphoreType.DMA((4,)),
            pltpu.SemaphoreType.DMA((8,)),
            *[pltpu.VMEM(source_now.shape, f32)] * 5,
            pltpu.SMEM(wavelet.shape, f32),
            pltpu.VMEM(traces.shape, f32),
            pltpu.VMEM(arrays[8].shape, jnp.int32),
        ],
        compiler_params=pltpu.CompilerParams(
            collective_id=0, has_side_effects=True, vmem_limit_bytes=24 << 20
        ),
    )(
        *[
            array if i == 6 else pltpu.with_memory_space_constraint(array, pltpu.HBM)
            for i, array in enumerate(arrays[:9])
        ]
    )
    return pl.pallas_call(
        functools.partial(finish, total_steps),
        out_shape=(
            field,
            field,
            field,
            field,
            jax.ShapeDtypeStruct(stored.shape, jnp.bfloat16),
            field,
        ),
        in_specs=[vmem, smem, vmem, vmem],
        out_specs=[vmem] * 6,
        compiler_params=pltpu.CompilerParams(vmem_limit_bytes=24 << 20),
    )(hist, plan, stored, arrays[11])


def solution(mesh):
    block = P(("shot", "gx"), "gy", None)
    kept = P("shot", "gx", "gy", None)
    return jax.shard_map(
        body,
        mesh=mesh,
        in_specs=(
            block,
            block,
            block,
            block,
            block,
            P("shot"),
            P("shot"),
            P("shot", ("gx", "gy")),
            P("shot", ("gx", "gy")),
            P("shot"),
            kept,
            block,
        ),
        out_specs=(block, block, block, block, kept, block),
        check_vma=False,
    )
```
